128 devices in a mesh: scan: 16 (over z, y), row: 8 (over x, core).
Axes of the slice: x: 4, y: 4, z: 4, core: 2. Of those that a mesh axis runs over, the one named last changes fastest.
Arguments:
- raw_planes: float32 [32, 6, 128, 1024], P('scan', None, 'row'), may hold values from 0 to 4
- shear_tiles: int32 [32], P('scan'), may hold values from 0 to 5, as said below
- axial_kernel: float32 [64], replicated, may hold values from 0.05 to 1
- column_kernel: float32 [31], replicated, may hold values from 0.05 to 1
- row_kernel: float32 [31], replicated, may hold values from 0.05 to 1
Outputs:
- estimate: float32 [32, 16, 128, 1024], P(None, 'scan', 'row')
The draws below stay inside these ranges and needn't reach their ends.
Inputs may be any that keep to these rules, and one draw needn't show every extreme that they name: `shear_tiles`: plane p has a shear within one tile of p * 5 // 31; the first plane has 0 and the last 5.
All inputs are finite; a program needn't handle non-finite values.
Results may differ from the reference program's by a relative error of at most 0.0003.
Values sent between devices are 32-bit elements; how exact they have to be, the bound alone decides.
A program may use at most 128 MiB of HBM per device.

```python
import math
import jax
import jax.numpy as jnp
from jax import lax

WIDTH = 1024
TILES = 6
TILE = 128
AXIAL_TAPS = 64
LATERAL_TAPS = 31
ITERS = 2
PLANES = 32
OUT_TILES = 16
SHIFT_MAX = 5


def draw_shear_tiles(key, part):
    indices = jnp.arange(PLANES, dtype=jnp.int32)
    base_value = indices * SHIFT_MAX // (PLANES - 1)
    jitter = jax.random.randint(key, (PLANES,), -1, 2, dtype=jnp.int32)
    value = jnp.clip(base_value + jitter, 0, SHIFT_MAX)
    value = jnp.where(indices == 0, 0, value)
    value = jnp.where(indices == PLANES - 1, SHIFT_MAX, value)
    return value.astype(jnp.int32)


def block_scale(rng, shape, cuts, low, high):
    factor_of = 1.0
    for dim, parts in cuts:
        heights = jax.random.uniform(jax.random.fold_in(jax.random.fold_in(rng, 6), dim), (parts,), jnp.float32, low / len(cuts), high / len(cuts))
        factor_of = factor_of * jnp.repeat(jnp.exp(heights), shape[dim] // parts).reshape((-1,) + (1,) * (len(shape) - 1 - dim))
    return factor_of


def setup_inputs(seed: int = 0) -> dict:
    splits = jax.random.split(jax.random.key(seed), 6)
    return {
        "raw_planes": jnp.clip(4.0 * jax.random.uniform(splits[0], (PLANES, TILES, TILE, WIDTH), jnp.float32) ** block_scale(splits[0], (PLANES, TILES, TILE, WIDTH), ((0, 16), (2, 8)), -0.2, 0.2), 0.0, 4.0),
        "shear_tiles": draw_shear_tiles(jax.random.fold_in(splits[5], 71), 0),
        "axial_kernel": jnp.clip(jnp.exp(jax.random.uniform(splits[2], (AXIAL_TAPS,), jnp.float32, math.log(0.05), math.log(1.0))), 0.05, 1.0),
        "column_kernel": jnp.clip(jnp.exp(jax.random.uniform(splits[3], (LATERAL_TAPS,), jnp.float32, math.log(0.05), math.log(1.0))), 0.05, 1.0),
        "row_kernel": jnp.clip(jnp.exp(jax.random.uniform(splits[4], (LATERAL_TAPS,), jnp.float32, math.log(0.05), math.log(1.0))), 0.05, 1.0),
    }


background_level = 0.5


def normalized(kernel):
    return kernel / jnp.sum(kernel)


def band_matrix(kernel, extent):
    length = kernel.shape[0]
    centre = length // 2
    indices = jnp.arange(extent, dtype=jnp.int32)
    offset = indices[None, :] - indices[:, None] + centre
    inside = (offset >= 0) & (offset < length)
    return jnp.where(inside, kernel[jnp.clip(offset, 0, length - 1)], 0.0)


def shifted_sum(volume, kernel, centre, axis):
    length = kernel.shape[0]
    extent = volume.shape[axis]
    widths = [(0, 0)] * volume.ndim
    widths[axis] = (centre, length - 1 - centre)
    padded = jnp.pad(volume, widths)
    summed = jnp.zeros_like(volume)
    for tap in range(length):
        summed = summed + kernel[tap] * lax.slice_in_dim(padded, tap, tap + extent, axis=axis)
    return summed


def spread_planes(tiles_in, shear_tiles, total):
    def place_plane(one_plane, offset):
        empty_slab = jnp.zeros((total,) + one_plane.shape[1:], one_plane.dtype)
        anchor = jnp.zeros((), jnp.int32)
        return lax.dynamic_update_slice(empty_slab, one_plane, (offset.astype(jnp.int32), anchor, anchor))
    return jax.vmap(place_plane)(tiles_in, shear_tiles)


def reference(raw_planes, shear_tiles, axial_kernel, column_kernel, row_kernel):
    axial = normalized(axial_kernel)
    across = normalized(column_kernel)
    down = normalized(row_kernel)
    lateral_len = across.shape[0]
    lateral_centre = lateral_len // 2
    spread = spread_planes(raw_planes, shear_tiles, OUT_TILES)
    data = spread.reshape(PLANES, OUT_TILES * TILE, WIDTH)
    estimate = data + 1.0
    matrix = band_matrix(axial, PLANES)

    def forward_plane(pair):
        data_plane, blurred_plane = pair
        blurred_plane = shifted_sum(blurred_plane, across, lateral_centre, 1)
        blurred_plane = shifted_sum(blurred_plane, down, lateral_centre, 0)
        quotient = data_plane / (blurred_plane + background_level)
        quotient = shifted_sum(quotient, down[::-1], lateral_len - 1 - lateral_centre, 0)
        return shifted_sum(quotient, across[::-1], lateral_len - 1 - lateral_centre, 1)

    for iteration in range(ITERS):
        blurred = jnp.tensordot(matrix, estimate, axes=1, precision=lax.Precision.HIGHEST)
        correction = lax.map(forward_plane, (data, blurred))
        correction = jnp.tensordot(matrix.T, correction, axes=1, precision=lax.Precision.HIGHEST)
        estimate = estimate * correction
    return estimate.reshape(PLANES, OUT_TILES, TILE, WIDTH)
```

```python
import jax
import jax.numpy as jnp
from jax import lax
from jax.experimental import pallas as pl
from jax.experimental.pallas import tpu as pltpu
from jax.sharding import PartitionSpec as P

PLANES = 32
TILES = 6
WINDOW = 8
LAST_TILE = 10
ROWS = 64
COLS = 256
HALO = 16
ITERS = 2
BACKGROUND = 0.5
F32 = jnp.float32
BF16 = jnp.bfloat16
MESH = pl.DeviceIdType.MESH
UP, DOWN, LEFT, RIGHT, LEFT_UP, LEFT_DOWN, RIGHT_UP, RIGHT_DOWN = range(8)


def split(value):
    high = value.astype(BF16)
    low = (value - high.astype(F32)).astype(BF16)
    return high, low


def dot(a, b):
    return jnp.dot(a, b, preferred_element_type=F32)


def dot3(a, b):
    return dot(a[0], b[0]) + (dot(a[0], b[1]) + dot(a[1], b[0]))


def iota(shape, axis):
    return lax.broadcasted_iota(jnp.int32, shape, axis)


def pick(taps, count, index):
    value = jnp.zeros(index.shape, F32)
    for tap in range(count):
        value = jnp.where(index == tap, taps[tap], value)
    return value


def plane_base(plane):
    return (plane * 5) // 31


def body(raw, shear, ax_s, co_s, ro_s, ax_v, co_v, ro_v, out,
         win, data, est, quo, mid, up, down, left, right, send_left, send_right,
         band_d, band_w, band_h, band_a, strips,
         d_send, d_recv, e_send, e_recv, t_send, t_recv):
    scan = lax.axis_index("scan")
    row = lax.axis_index("row")
    x = row // 2
    core = row % 2
    block = 2 * scan + core

    for n in range(2):
        delta = shear[n] - plane_base(2 * scan + n)
        for k in range(WINDOW):
            zero = jnp.zeros(raw.shape[2:], F32)
            early = raw[n, k] if k < TILES else zero
            level = raw[n, k - 1] if 1 <= k <= TILES else zero
            late = raw[n, k - 2] if k >= 2 else zero
            win[n, k] = jnp.where(delta == 0, level, jnp.where(delta < 0, early, late))

    def deskew_copies(n, k, cb):
        plane = 2 * scan + n
        tile = plane_base(plane) - 1 + k
        half = x // 2
        offset = 32 * (x % 2) + 16 * core
        source = win.at[n, k, :, pl.ds(256 * cb, 256)]
        target = data.at[plane, pl.ds(pl.multiple_of(offset, 16), 16), :]
        real = jnp.logical_and(tile >= 0, tile <= LAST_TILE)
        mine = jnp.logical_and(tile == scan, jnp.logical_and(cb == x, half == core))
        remote = pltpu.make_async_remote_copy(
            src_ref=source, dst_ref=target, send_sem=d_send.at[n, k, cb], recv_sem=d_recv.at[plane],
            device_id=(tile, 2 * cb + half), device_id_type=MESH)
        local = pltpu.make_async_copy(source, target, d_recv.at[plane])
        return jnp.logical_and(real, mine), local, jnp.logical_and(real, jnp.logical_not(mine)), remote

    for n in range(2):
        for k in range(WINDOW):
            for cb in range(4):
                is_local, local, is_remote, remote = deskew_copies(n, k, cb)
                pl.when(is_local)(local.start)
                pl.when(is_remote)(remote.start)

    for way in range(2):
        sign = 1 if way == 0 else -1
        total = jnp.sum(ro_v[...], axis=1, keepdims=True)
        shape = (ROWS, ROWS + 2 * HALO)
        step = iota(shape, 1) - HALO - iota(shape, 0)
        high, low = split(pick(ro_s, 31, sign * step + 15) / total)
        band_d[way, 0], band_d[way, 1] = high, low

        total = jnp.sum(co_v[...], axis=1, keepdims=True)
        @pl.loop(0, 16)
        def _(b):
            shape = (16, COLS)
            start = pl.multiple_of(b * 16, 16)
            step = start + iota(shape, 0) - iota(shape, 1)
            high, low = split(pick(co_s, 31, sign * step + 15) / total)
            band_w[way, 0, pl.ds(start, 16), :] = high
            band_w[way, 1, pl.ds(start, 16), :] = low
        shape = (16, COLS)
        step = iota(shape, 0) - HALO - iota(shape, 1)
        left_band = split(pick(co_s, 31, sign * step + 15) / total)
        step = iota(shape, 0) + COLS - iota(shape, 1)
        right_band = split(pick(co_s, 31, sign * step + 15) / total)
        for part in range(2):
            band_h[way, part] = jnp.zeros((8, 2 * 128, COLS), BF16)
            for g in range(8):
                slot = 16 * ((g + 7) % 8)
                band_h[way, part, g, slot:slot + 16, :] = left_band[part]
                slot = 128 + 16 * g
                band_h[way, part, g, slot:slot + 16, :] = right_band[part]

        total = jnp.sum(ax_v[...], axis=1, keepdims=True)
        @pl.loop(0, 16)
        def _(b):
            shape = (16, 256)
            start = pl.multiple_of(b * 16, 16)
            i = start + iota(shape, 0)
            j = iota(shape, 1)
            step = jnp.where(i % 8 == j % 8, j // 8 - i // 8, -100)
            if way == 0:
                index = step + 32
            else:
                index = jnp.where(step > -50, 32 - step, -1)
            high, low = split(pick(ax_s, 64, index) / total)
            band_a[way, 0, pl.ds(start, 16), :] = high
            band_a[way, 1, pl.ds(start, 16), :] = low

    @pl.loop(0, PLANES)
    def _(plane):
        base = plane_base(plane)
        here = jnp.logical_and(jnp.logical_and(scan >= base - 1, scan <= base + 6), scan <= LAST_TILE)
        @pl.when(here)
        def _():
            pltpu.make_async_copy(data.at[plane], data.at[plane], d_recv.at[plane]).wait()
        @pl.when(jnp.logical_not(here))
        def _():
            data[plane] = jnp.zeros((ROWS, COLS), F32)

    @pl.loop(0, PLANES)
    def _(plane):
        est[plane] = data[plane] + 1.0

    lane = iota((ROWS, 128), 1)

    def exchange(e, volume):
        def place(d_block, d_x):
            other = block + d_block
            return (other // 2, 2 * (x + d_x) + other % 2)

        def copy(way, source, target, d_block, d_x):
            exists = jnp.logical_and(jnp.logical_and(block + d_block >= 0, block + d_block < 32),
                                     jnp.logical_and(x + d_x >= 0, x + d_x < 4))
            comes = jnp.logical_and(jnp.logical_and(block - d_block >= 0, block - d_block < 32),
                                    jnp.logical_and(x - d_x >= 0, x - d_x < 4))
            return exists, comes, target, pltpu.make_async_remote_copy(
                src_ref=source, dst_ref=target, send_sem=e_send.at[e, way], recv_sem=e_recv.at[e, way],
                device_id=place(d_block, d_x), device_id_type=MESH)

        first, last = pl.ds(0, HALO), pl.ds(ROWS - HALO, HALO)
        own = pl.ds(HALO, ROWS)
        before, after = pl.ds(0, HALO), pl.ds(HALO + ROWS, HALO)
        rows = [
            copy(UP, volume.at[:, first, :], down.at[e], -1, 0),
            copy(DOWN, volume.at[:, last, :], up.at[e], 1, 0),
        ]
        for exists, _, _, c in rows:
            pl.when(exists)(c.start)

        @pl.loop(0, 4)
        def _(j):
            packed_left = jnp.zeros((ROWS, 128), F32)
            packed_right = jnp.zeros((ROWS, 128), F32)
            for g in range(8):
                ends = jnp.where(lane < 64, volume[4 * g + j, :, 0:128], volume[4 * g + j, :, 128:256])
                if g:
                    ends = pltpu.roll(ends, 16 * g, 1)
                packed_left = jnp.where(lane // 16 == g, ends, packed_left)
                packed_right = jnp.where(lane // 16 == (g + 7) % 8, ends, packed_right)
            send_left[e, j] = packed_left
            send_right[e, j] = packed_right

        sides = [
            copy(LEFT, send_left.at[e], right.at[e, :, own, :], 0, -1),
            copy(RIGHT, send_right.at[e], left.at[e, :, own, :], 0, 1),
            copy(LEFT_UP, send_left.at[e, :, first, :], right.at[e, :, after, :], -1, -1),
            copy(LEFT_DOWN, send_left.at[e, :, last, :], right.at[e, :, before, :], 1, -1),
            copy(RIGHT_UP, send_right.at[e, :, first, :], left.at[e, :, after, :], -1, 1),
            copy(RIGHT_DOWN, send_right.at[e, :, last, :], left.at[e, :, before, :], 1, 1),
        ]
        for exists, _, _, c in sides:
            pl.when(exists)(c.start)
        for _, comes, target, c in rows + sides:
            pl.when(comes)(c.wait_recv)
            @pl.when(jnp.logical_not(comes))
            def _():
                target[...] = jnp.zeros(target.shape, F32)
        return [(exists, c) for exists, _, _, c in rows + sides]

    def blur(e, way, volume, finish):
        down_band = (band_d[way, 0], band_d[way, 1])

        @pl.loop(0, 4)
        def _(j):
            values = jnp.concatenate([left[e, j], right[e, j]], axis=1)
            high, low = split(dot3(down_band, split(values)))
            start = pl.multiple_of(j * ROWS, ROWS)
            strips[0, pl.ds(start, ROWS), :] = high
            strips[1, pl.ds(start, ROWS), :] = low

        @pl.loop(0, 8)
        def _(g):
            parts = []
            for j in range(4):
                plane = 4 * g + j
                values = jnp.concatenate([up[e, plane], volume[plane], down[e, plane]], axis=0)
                parts.append(dot3(down_band, split(values)))
            own = split(jnp.concatenate(parts, axis=0))
            result = dot3(own, (band_w[way, 0], band_w[way, 1]))
            result += dot3((strips[0], strips[1]), (band_h[way, 0, g], band_h[way, 1, g]))
            mid[pl.ds(4 * g, 4)] = result.reshape(4, ROWS, COLS)

        axial = (band_a[way, 0], band_a[way, 1])

        def axial_rows(b):
            start = pl.multiple_of(8 * b, 8)
            where = pl.ds(start, 8)
            values = mid[:, where, :].reshape(256, COLS)
            finish(where, dot3(axial, split(values)).reshape(PLANES, 8, COLS))

        return axial_rows

    def to_quotient(where, blurred):
        quo[:, where, :] = data[:, where, :] / (blurred + BACKGROUND)

    def to_estimate(where, correction):
        est[:, where, :] = est[:, where, :] * correction

    for it in range(ITERS):
        sent_est = exchange(2 * it, est)
        forward = blur(2 * it, 0, est, to_quotient)
        if it:
            for exists, c in sent_quo:
                pl.when(exists)(c.wait_send)
        pl.loop(0, 8)(forward)
        sent_quo = exchange(2 * it + 1, quo)
        backward = blur(2 * it + 1, 1, quo, to_estimate)
        for exists, c in sent_est:
            pl.when(exists)(c.wait_send)
        if it < ITERS - 1:
            pl.loop(0, 8)(backward)

    pieces = []
    columns = pl.ds(pl.multiple_of(256 * x, 256), 256)
    for i in range(4):
        backward(2 * i)
        backward(2 * i + 1)
        owner = 4 * core + i
        source = est.at[:, pl.ds(16 * i, 16), :]
        target = out.at[:, :, columns]
        remote = pltpu.make_async_remote_copy(
            src_ref=source, dst_ref=target, send_sem=t_send.at[i], recv_sem=t_recv.at[x],
            device_id=(scan, owner), device_id_type=MESH)
        local = pltpu.make_async_copy(source, target, t_recv.at[x])
        pl.when(owner == row)(local.start)
        pl.when(owner != row)(remote.start)
        pieces.append((owner != row, remote))
    for i in range(4):
        target = out.at[:, :, pl.ds(256 * i, 256)]
        pltpu.make_async_copy(target, target, t_recv.at[i]).wait()

    for exists, c in pieces + sent_quo:
        pl.when(exists)(c.wait_send)
    for n in range(2):
        for k in range(WINDOW):
            for cb in range(4):
                _, _, is_remote, remote = deskew_copies(n, k, cb)
                pl.when(is_remote)(remote.wait_send)


def shards(raw_planes, shear_tiles, axial_kernel, column_kernel, row_kernel):
    raw = raw_planes.reshape(2, TILES, 16, 1024)
    taps = (axial_kernel, column_kernel, row_kernel)
    vmem = pl.BlockSpec(memory_space=pltpu.VMEM)
    smem = pl.BlockSpec(memory_space=pltpu.SMEM)
    half = (ITERS * 2, PLANES, HALO, COLS)
    strip = (ITERS * 2, 4, ROWS + 2 * HALO, 128)
    out = pl.pallas_call(
        body,
        out_shape=jax.ShapeDtypeStruct((PLANES, 16, 1024), F32),
        in_specs=[vmem, smem, smem, smem, smem, vmem, vmem, vmem],
        out_specs=pl.BlockSpec(memory_space=pl.ANY),
        scratch_shapes=[
            pltpu.VMEM((2, WINDOW, 16, 1024), F32),
            pltpu.VMEM((PLANES, ROWS, COLS), F32),
            pltpu.VMEM((PLANES, ROWS, COLS), F32),
            pltpu.VMEM((PLANES, ROWS, COLS), F32),
            pltpu.VMEM((PLANES, ROWS, COLS), F32),
            pltpu.VMEM(half, F32),
            pltpu.VMEM(half, F32),
            pltpu.VMEM(strip, F32),
            pltpu.VMEM(strip, F32),
            pltpu.VMEM((ITERS * 2, 4, ROWS, 128), F32),
            pltpu.VMEM((ITERS * 2, 4, ROWS, 128), F32),
            pltpu.VMEM((2, 2, ROWS, ROWS + 2 * HALO), BF16),
            pltpu.VMEM((2, 2, COLS, COLS), BF16),
            pltpu.VMEM((2, 2, 8, 256, COLS), BF16),
            pltpu.VMEM((2, 2, 256, 256), BF16),
            pltpu.VMEM((2, 4 * ROWS, 256), BF16),
            pltpu.SemaphoreType.DMA((2, WINDOW, 4)),
            pltpu.SemaphoreType.DMA((PLANES,)),
            pltpu.SemaphoreType.DMA((ITERS * 2, 8)),
            pltpu.SemaphoreType.DMA((ITERS * 2, 8)),
            pltpu.SemaphoreType.DMA((4,)),
            pltpu.SemaphoreType.DMA((4,)),
        ],
        compiler_params=pltpu.CompilerParams(has_side_effects=True, vmem_limit_bytes=48 << 20),
        name="deconvolve",
    )(raw, shear_tiles, *taps, *(t.reshape(1, -1) for t in taps))
    return out.reshape(PLANES, 1, 16, 1024)


def solution(mesh):
    return jax.shard_map(
        shards,
        mesh=mesh,
        in_specs=(P("scan", None, "row", None), P("scan"), P(), P(), P()),
        out_specs=P(None, "scan", "row", None),
        check_vma=False,
    )
```

```python
import jax
import jax.numpy as jnp
from jax import lax
from jax.experimental import pallas as pl
from jax.experimental.pallas import tpu as pltpu
from jax.sharding import PartitionSpec as P

PLANES = 32
TILES = 6
WINDOW = 8
LAST_TILE = 10
ROWS = 64
COLS = 256
HALO = 16
ITERS = 2
BACKGROUND = 0.5
F32 = jnp.float32
BF16 = jnp.bfloat16
MESH = pl.DeviceIdType.MESH
UP, DOWN, LEFT, RIGHT, LEFT_UP, LEFT_DOWN, RIGHT_UP, RIGHT_DOWN = range(8)


def split(value):
    high = value.astype(BF16)
    low = (value - high.astype(F32)).astype(BF16)
    return high, low


def dot(a, b):
    return jnp.dot(a, b, preferred_element_type=F32)


def iota(shape, axis):
    return lax.broadcasted_iota(jnp.int32, shape, axis)


def pick(taps, count, index):
    value = jnp.zeros(index.shape, F32)
    for tap in range(count):
        value = jnp.where(index == tap, taps[tap], value)
    return value


def plane_base(plane):
    return (plane * 5) // 31


def body(raw_in, shear_in, ax_in, co_in, ro_in, out,
         raw, shear, ax_s, co_s, ro_s, win, data, est, quo, mid, up, down, left, right, send_left, send_right,
         band_d, band_w, band_a, masks, parts,
         in_sem, d_send, d_recv, e_send, e_recv, t_send, t_recv):
    scan = lax.axis_index("scan")
    row = lax.axis_index("row")
    x = row // 2
    core = row % 2
    block = 2 * scan + core
    half = x // 2

    loads = [pltpu.make_async_copy(a, b, in_sem.at[i]) for i, (a, b) in enumerate(
        [(shear_in, shear), (raw_in.at[0], raw.at[0]), (raw_in.at[1], raw.at[1]), (ax_in, ax_s), (co_in, co_s), (ro_in, ro_s)])]
    for load in loads:
        load.start()

    barrier = pltpu.get_barrier_semaphore()

    def inside(d_block, d_x):
        return jnp.logical_and(jnp.logical_and(block + d_block >= 0, block + d_block < 32),
                               jnp.logical_and(x + d_x >= 0, x + d_x < 4))

    def place(d_block, d_x):
        other = block + d_block
        return (other // 2, 2 * (x + d_x) + other % 2)

    def greet(condition, device):
        @pl.when(condition)
        def _():
            pl.semaphore_signal(barrier, inc=1, device_id=device, device_id_type=MESH)

    def window(source):
        first = plane_base(2 * source) - 1
        last = plane_base(2 * source + 1) + 6
        return jnp.maximum(first, 0), jnp.minimum(last, LAST_TILE)

    @pl.loop(0, 16)
    def _(source):
        first, last = window(source)
        sends = jnp.logical_and(scan >= first, scan <= last)
        for i in range(4):
            other = 4 * core + i
            greet(jnp.logical_and(sends, jnp.logical_or(source != scan, other != row)), (source, other))

    count = 0
    for d_block in (-1, 0, 1):
        for d_x in (-1, 0, 1):
            if d_block or d_x:
                greet(inside(d_block, d_x), place(d_block, d_x))
                count = count + inside(d_block, d_x).astype(jnp.int32)
    for i in range(4):
        other = 2 * i + row // 4
        greet(other != row, (scan, other))
    first, last = window(scan)
    count = count + 4 * (last - first + 1)
    to_self = jnp.logical_and(jnp.logical_and(scan >= first, scan <= last), half == core)
    count = count - to_self.astype(jnp.int32)
    count = count + 4 - (row // 4 == core).astype(jnp.int32)

    loads[0].wait()
    for n in range(2):
        loads[1 + n].wait()
        delta = shear[n] - plane_base(2 * scan + n)
        for k in range(WINDOW):
            zero = jnp.zeros(raw.shape[2:], F32)
            early = raw[n, k] if k < TILES else zero
            level = raw[n, k - 1] if 1 <= k <= TILES else zero
            late = raw[n, k - 2] if k >= 2 else zero
            win[n, k] = jnp.where(delta == 0, level, jnp.where(delta < 0, early, late))

    def deskew_copies(n, i, j):
        plane = 2 * scan + n
        k = (scan + i) % WINDOW
        cb = (x + j) % 4
        tile = plane_base(plane) - 1 + k
        offset = 32 * (x % 2) + 16 * core
        source = win.at[n, k, :, pl.ds(pl.multiple_of(256 * cb, 256), 256)]
        target = data.at[plane, pl.ds(pl.multiple_of(offset, 16), 16), :]
        real = jnp.logical_and(tile >= 0, tile <= LAST_TILE)
        mine = jnp.logical_and(tile == scan, jnp.logical_and(cb == x, half == core))
        remote = pltpu.make_async_remote_copy(
            src_ref=source, dst_ref=target, send_sem=d_send.at[n, i, j], recv_sem=d_recv.at[plane],
            device_id=(tile, 2 * cb + half), device_id_type=MESH)
        return jnp.logical_and(real, mine), (source, target, d_recv.at[plane]), jnp.logical_and(real, jnp.logical_not(mine)), remote

    pl.semaphore_wait(barrier, count)
    for n in range(2):
        for i in range(WINDOW):
            for j in range(4):
                is_local, local, is_remote, remote = deskew_copies(n, i, j)
                if j == 0:
                    @pl.when(is_local)
                    def _():
                        pltpu.make_async_copy(*local).start()
                pl.when(is_remote)(remote.start)

    for load in loads[3:]:
        load.wait()

    def total_of(taps, n):
        total = taps[0]
        for k in range(1, n):
            total = total + taps[k]
        return total

    ax_total, co_total, ro_total = total_of(ax_s, 64), total_of(co_s, 31), total_of(ro_s, 31)
    span = ROWS + 2 * HALO
    group = iota((16, 256), 1) // 16
    for g in range(8):
        masks[g] = jnp.where(group < 8, jnp.where(group == (g + 7) % 8, 1.0, 0.0), jnp.where(group == g + 8, 1.0, 0.0)).astype(BF16)
    for way in range(2):
        sign = 1 if way == 0 else -1
        shape = (ROWS, span)
        step = iota(shape, 1) - HALO - iota(shape, 0)
        high, low = split(pick(ro_s, 31, sign * step + 15) / ro_total)
        band_d[way] = jnp.concatenate([
            jnp.concatenate([high, high], axis=1), jnp.concatenate([low, jnp.zeros(shape, BF16)], axis=1)], axis=0)

        shape = (16, COLS)

        @pl.loop(0, 16)
        def _(b):
            start = pl.multiple_of(b * 16, 16)
            step = start + iota(shape, 0) - iota(shape, 1)
            high, low = split(pick(co_s, 31, sign * step + 15) / co_total)
            band_w[way, 0, pl.ds(start, 16), :] = high
            band_w[way, 1, pl.ds(start, 16), :] = low
        step = iota(shape, 0) - HALO - iota(shape, 1)
        left_band = split(pick(co_s, 31, sign * step + 15) / co_total)
        step = iota(shape, 0) + COLS - iota(shape, 1)
        right_band = split(pick(co_s, 31, sign * step + 15) / co_total)
        for part in range(2):
            for g in range(8):
                band_w[way, part, 256 + 16 * g:272 + 16 * g, :] = left_band[part]
                band_w[way, part, 384 + 16 * g:400 + 16 * g, :] = right_band[part]

        @pl.loop(0, 16)
        def _(b):
            start = pl.multiple_of(b * 16, 16)
            i = start + iota(shape, 0)
            j = iota(shape, 1)
            step = j // 8 - i // 8
            index = jnp.where(i % 8 == j % 8, sign * step + 32, -1)
            high, low = split(pick(ax_s, 64, index) / ax_total)
            band_a[way, pl.ds(start, 16), :] = jnp.concatenate([high, high, low], axis=1)

    first, last = pl.ds(0, HALO), pl.ds(ROWS - HALO, HALO)
    own = pl.ds(HALO, ROWS)
    before, after = pl.ds(0, HALO), pl.ds(HALO + ROWS, HALO)

    def row_copies(e, volume, planes):
        return [
            (UP, volume.at[planes, first, :], down.at[e, planes], -1, 0),
            (DOWN, volume.at[planes, last, :], up.at[e, planes], 1, 0),
        ]

    def side_copies(e, h):
        return [
            (LEFT, send_left.at[e, h], right.at[e, h, own, :], 0, -1),
            (RIGHT, send_right.at[e, h], left.at[e, h, own, :], 0, 1),
            (LEFT_UP, send_left.at[e, h, first, :], right.at[e, h, after, :], -1, -1),
            (LEFT_DOWN, send_left.at[e, h, last, :], right.at[e, h, before, :], 1, -1),
            (RIGHT_UP, send_right.at[e, h, first, :], left.at[e, h, after, :], -1, 1),
            (RIGHT_DOWN, send_right.at[e, h, last, :], left.at[e, h, before, :], 1, 1),
        ]

    def descriptor(e, h, way, source, target, d_block, d_x):
        return pltpu.make_async_remote_copy(
            src_ref=source, dst_ref=target, send_sem=e_send.at[e, way], recv_sem=e_recv.at[e, h, way],
            device_id=place(d_block, d_x), device_id_type=MESH)

    def chunk(h):
        return pl.ds(8 * h, 8)

    def start(e, h, copies):
        for c in copies:
            pl.when(inside(c[3], c[4]))(descriptor(e, h, *c).start)

    def arrive(e, h, volume):
        for c in row_copies(e, volume, chunk(h)) + side_copies(e, h):
            comes = inside(-c[3], -c[4])
            pl.when(comes)(descriptor(e, h, *c).wait_recv)
            @pl.when(jnp.logical_not(comes))
            def _():
                c[2][...] = jnp.zeros(c[2].shape, F32)

    def drain(e, volume):
        every = slice(None)
        for c in row_copies(e, volume, every) + side_copies(e, every):
            pl.when(inside(c[3], c[4]))(descriptor(e, 0, *c).wait_send)

    lane = iota((ROWS, 128), 1)

    def pack(e, h, volume):
        packed_left = jnp.zeros((ROWS, 128), F32)
        packed_right = jnp.zeros((ROWS, 128), F32)
        for g in range(8):
            ends = jnp.where(lane < 64, volume[8 * h + g, :, 0:128], volume[8 * h + g, :, 128:256])
            if g:
                ends = pltpu.roll(ends, 16 * g, 1)
            packed_left = jnp.where(lane // 16 == g, ends, packed_left)
            packed_right = jnp.where(lane // 16 == (g + 7) % 8, ends, packed_right)
        send_left[e, h] = packed_left
        send_right[e, h] = packed_right

    def along_rows(way, values):
        high, low = split(values)
        both = dot(band_d[way], jnp.concatenate([high, low], axis=0))
        return split(both[:ROWS] + both[ROWS:])

    def lateral(e, way, volume, h):
        strip = along_rows(way, jnp.concatenate([left[e, h], right[e, h]], axis=1))
        for g in range(8):
            plane = 8 * h + g
            high, low = along_rows(way, jnp.concatenate([up[e, plane], volume[plane], down[e, plane]], axis=0))
            here = pl.ds(ROWS * g, ROWS)
            parts[here, 0:256] = high
            parts[here, 256:512] = low
            for part in range(2):
                kept = strip[part].reshape(4, 16, 256) * masks[g][None]
                parts[here, 512 + 256 * part:768 + 256 * part] = kept.reshape(ROWS, 256)
        high, low = parts[:, 0:256], parts[:, 256:512]
        side_high, side_low = parts[:, 512:768], parts[:, 768:1024]
        values = jnp.concatenate([high, side_high, low, side_low, high, side_high], axis=1)
        bands = jnp.concatenate([band_w[way, 0], band_w[way, 0], band_w[way, 1]], axis=0)
        mid[chunk(h)] = dot(values, bands).reshape(8, ROWS, COLS)

    def axial(way, b):
        where = pl.ds(pl.multiple_of(8 * b, 8), 8)
        high, low = split(mid[:, where, :].reshape(256, COLS))
        value = dot(band_a[way], jnp.concatenate([high, low, high], axis=0)).reshape(PLANES, 8, COLS)
        if way == 0:
            quo[:, where, :] = data[:, where, :] / (value + BACKGROUND)
        else:
            est[:, where, :] = est[:, where, :] * value

    def axial_and_send(way, e, volume):
        @pl.loop(0, 4)
        def _(b):
            axial(way, b + 4 * (b // 2))

        @pl.loop(0, 4)
        def _(h):
            start(e, h, row_copies(e, volume, chunk(h)))

        @pl.loop(2, 6)
        def _(b):
            axial(way, b)

        @pl.loop(0, 4)
        def _(h):
            pack(e, h, volume)
            start(e, h, side_copies(e, h))

    def lateral_all(e, way, volume):
        @pl.loop(0, 4)
        def _(h):
            arrive(e, h, volume)
            lateral(e, way, volume, h)

    ring = scan // 4

    def turn(o):
        return (ring + o + o // 2 - 2 * (o // 3)) % 4

    @pl.loop(0, 5)
    def _(o):
        @pl.when(o < 4)
        def _():
            h = turn(o)
            for g in range(8):
                plane = 8 * h + g
                base = plane_base(plane)
                here = jnp.logical_and(jnp.logical_and(scan >= base - 1, scan <= base + 6), scan <= LAST_TILE)
                @pl.when(here)
                def _():
                    pltpu.make_async_copy(data.at[plane], data.at[plane], d_recv.at[plane]).wait()
                @pl.when(jnp.logical_not(here))
                def _():
                    data[plane] = jnp.zeros((ROWS, COLS), F32)
                est[plane] = data[plane] + 1.0
            start(0, h, row_copies(0, est, chunk(h)))
            pack(0, h, est)
            start(0, h, side_copies(0, h))

        @pl.when(o > 0)
        def _():
            h = turn(o - 1)
            arrive(0, h, est)
            lateral(0, 0, est, h)

    axial_and_send(0, 1, quo)
    lateral_all(1, 1, quo)
    drain(0, est)
    axial_and_send(1, 2, est)
    lateral_all(2, 0, est)
    drain(1, quo)
    axial_and_send(0, 3, quo)
    lateral_all(3, 1, quo)
    drain(2, est)

    pieces = []
    columns = pl.ds(pl.multiple_of(256 * x, 256), 256)
    for i in range(4):
        axial(1, 2 * i)
        axial(1, 2 * i + 1)
        owner = 4 * core + i
        source = est.at[:, pl.ds(16 * i, 16), :]
        target = out.at[:, :, columns]
        remote = pltpu.make_async_remote_copy(
            src_ref=source, dst_ref=target, send_sem=t_send.at[i], recv_sem=t_recv.at[x],
            device_id=(scan, owner), device_id_type=MESH)
        @pl.when(owner == row)
        def _():
            pltpu.make_async_copy(source, target, t_recv.at[x]).start()
        pl.when(owner != row)(remote.start)
        pieces.append((owner != row, remote))
    drain(3, quo)
    for n in range(2):
        for i in range(WINDOW):
            for j in range(4):
                _, _, is_remote, remote = deskew_copies(n, i, j)
                pl.when(is_remote)(remote.wait_send)
    for i in range(4):
        target = out.at[:, :, pl.ds(256 * i, 256)]
        pltpu.make_async_copy(target, target, t_recv.at[i]).wait()
    for exists, c in pieces:
        pl.when(exists)(c.wait_send)


def shards(raw_planes, shear_tiles, axial_kernel, column_kernel, row_kernel):
    raw = raw_planes.reshape(2, TILES, 16, 1024)
    hbm = pl.BlockSpec(memory_space=pltpu.HBM)
    half = (ITERS * 2, PLANES, HALO, COLS)
    strip = (ITERS * 2, 4, ROWS + 2 * HALO, 128)
    volume = pltpu.VMEM((PLANES, ROWS, COLS), F32)
    out = pl.pallas_call(
        body,
        out_shape=jax.ShapeDtypeStruct((PLANES, 16, 1024), F32),
        in_specs=[hbm] * 5,
        out_specs=pl.BlockSpec(memory_space=pl.ANY),
        scratch_shapes=[
            pltpu.VMEM((2, TILES, 16, 1024), F32),
            pltpu.SMEM((2,), jnp.int32),
            pltpu.SMEM((64,), F32),
            pltpu.SMEM((31,), F32),
            pltpu.SMEM((31,), F32),
            pltpu.VMEM((2, WINDOW, 16, 1024), F32),
            volume, volume, volume, volume,
            pltpu.VMEM(half, F32),
            pltpu.VMEM(half, F32),
            pltpu.VMEM(strip, F32),
            pltpu.VMEM(strip, F32),
            pltpu.VMEM((ITERS * 2, 4, ROWS, 128), F32),
            pltpu.VMEM((ITERS * 2, 4, ROWS, 128), F32),
            pltpu.VMEM((2, 2 * ROWS, 2 * (ROWS + 2 * HALO)), BF16),
            pltpu.VMEM((2, 2, 512, COLS), BF16),
            pltpu.VMEM((2, 256, 768), BF16),
            pltpu.VMEM((8, 16, 256), BF16),
            pltpu.VMEM((8 * ROWS, 1024), BF16),
            pltpu.SemaphoreType.DMA((6,)),
            pltpu.SemaphoreType.DMA((2, WINDOW, 4)),
            pltpu.SemaphoreType.DMA((PLANES,)),
            pltpu.SemaphoreType.DMA((ITERS * 2, 8)),
            pltpu.SemaphoreType.DMA((ITERS * 2, 4, 8)),
            pltpu.SemaphoreType.DMA((4,)),
            pltpu.SemaphoreType.DMA((4,)),
        ],
        compiler_params=pltpu.CompilerParams(collective_id=0, has_side_effects=True, vmem_limit_bytes=48 << 20),
        name="deconvolve",
    )(raw, shear_tiles, axial_kernel, column_kernel, row_kernel)
    return out.reshape(PLANES, 1, 16, 1024)


def solution(mesh):
    return jax.shard_map(
        shards,
        mesh=mesh,
        in_specs=(P("scan", None, "row", None), P("scan"), P(), P(), P()),
        out_specs=P(None, "scan", "row", None),
        check_vma=False,
    )
```

```python
import jax
import jax.numpy as jnp
from jax import lax
from jax.experimental import pallas as pl
from jax.experimental.pallas import tpu as pltpu
from jax.sharding import PartitionSpec as P

PLANES = 32
TILES = 6
WINDOW = 8
LAST_TILE = 10
ROWS = 64
COLS = 256
HALO = 16
ITERS = 2
BACKGROUND = 0.5
F32 = jnp.float32
BF16 = jnp.bfloat16
MESH = pl.DeviceIdType.MESH
UP, DOWN, LEFT, RIGHT, LEFT_UP, LEFT_DOWN, RIGHT_UP, RIGHT_DOWN = range(8)


def split(value):
    high = value.astype(BF16)
    low = (value - high.astype(F32)).astype(BF16)
    return high, low


def dot(a, b):
    return jnp.dot(a, b, preferred_element_type=F32)


def iota(shape, axis):
    return lax.broadcasted_iota(jnp.int32, shape, axis)


def pick(taps, count, index):
    value = jnp.zeros(index.shape, F32)
    for tap in range(count):
        value = jnp.where(index == tap, taps[tap], value)
    return value


def plane_base(plane):
    return (plane * 5) // 31


def body(raw_in, shear_in, ax_in, co_in, ro_in, out,
         raw, shear, ax_s, co_s, ro_s, win, data, est, quo, mid, up, down, left, right, send_left, send_right,
         band_d, band_w, band_a, masks, parts,
         in_sem, d_send, d_recv, e_send, e_recv, t_send, t_recv):
    scan = lax.axis_index("scan")
    row = lax.axis_index("row")
    x = row // 2
    core = row % 2
    block = 2 * scan + core
    half = x // 2
    ring = scan // 4

    loads = [pltpu.make_async_copy(a, b, in_sem.at[i]) for i, (a, b) in enumerate(
        [(shear_in, shear), (raw_in.at[0], raw.at[0]), (raw_in.at[1], raw.at[1]), (ax_in, ax_s), (co_in, co_s), (ro_in, ro_s)])]
    for load in loads:
        load.start()

    barrier = pltpu.get_barrier_semaphore()

    def inside(d_block, d_x):
        return jnp.logical_and(jnp.logical_and(block + d_block >= 0, block + d_block < 32),
                               jnp.logical_and(x + d_x >= 0, x + d_x < 4))

    def place(d_block, d_x):
        other = block + d_block
        return (other // 2, 2 * (x + d_x) + other % 2)

    def greet(condition, device):
        @pl.when(condition)
        def _():
            pl.semaphore_signal(barrier, inc=1, device_id=device, device_id_type=MESH)

    def window(source):
        first = plane_base(2 * source) - 1
        last = plane_base(2 * source + 1) + 6
        return jnp.maximum(first, 0), jnp.minimum(last, LAST_TILE)

    @pl.loop(0, 16)
    def _(source):
        first, last = window(source)
        sends = jnp.logical_and(scan >= first, scan <= last)
        for i in range(4):
            other = 4 * core + i
            greet(jnp.logical_and(sends, jnp.logical_or(source != scan, other != row)), (source, other))

    count = 0
    for d_block in (-1, 0, 1):
        for d_x in (-1, 0, 1):
            if d_block or d_x:
                greet(inside(d_block, d_x), place(d_block, d_x))
                count = count + inside(d_block, d_x).astype(jnp.int32)
    for i in range(4):
        other = 2 * i + row // 4
        greet(other != row, (scan, other))
    first, last = window(scan)
    count = count + 4 * (last - first + 1)
    to_self = jnp.logical_and(jnp.logical_and(scan >= first, scan <= last), half == core)
    count = count - to_self.astype(jnp.int32)
    count = count + 4 - (row // 4 == core).astype(jnp.int32)

    loads[0].wait()
    for n in range(2):
        loads[1 + n].wait()
        delta = shear[n] - plane_base(2 * scan + n)
        for k in range(WINDOW):
            zero = jnp.zeros(raw.shape[2:], F32)
            early = raw[n, k] if k < TILES else zero
            level = raw[n, k - 1] if 1 <= k <= TILES else zero
            late = raw[n, k - 2] if k >= 2 else zero
            win[n, k] = jnp.where(delta == 0, level, jnp.where(delta < 0, early, late))

    def deskew_copies(n, i, j):
        plane = 2 * scan + n
        base = plane_base(plane)
        tile = 4 * ((1 + ring % 2 + i // 4) % 3) + (i + scan) % 4
        cb = (x + j) % 4
        offset = 32 * (x % 2) + 16 * core
        source = win.at[n, jnp.clip(tile - base + 1, 0, WINDOW - 1), :, pl.ds(pl.multiple_of(256 * cb, 256), 256)]
        target = data.at[plane, pl.ds(pl.multiple_of(offset, 16), 16), :]
        real = jnp.logical_and(jnp.logical_and(tile >= base - 1, tile <= base + 6), tile <= LAST_TILE)
        mine = jnp.logical_and(tile == scan, jnp.logical_and(cb == x, half == core))
        remote = pltpu.make_async_remote_copy(
            src_ref=source, dst_ref=target, send_sem=d_send.at[n, i, j], recv_sem=d_recv.at[plane],
            device_id=(tile, 2 * cb + half), device_id_type=MESH)
        return jnp.logical_and(real, mine), (source, target, d_recv.at[plane]), jnp.logical_and(real, jnp.logical_not(mine)), remote

    pl.semaphore_wait(barrier, count)
    for i in range(12):
        for n in range(2):
            for j in range(4):
                is_local, local, is_remote, remote = deskew_copies(n, i, j)
                if j == 0:
                    @pl.when(is_local)
                    def _():
                        pltpu.make_async_copy(*local).start()
                pl.when(is_remote)(remote.start)

    for load in loads[3:]:
        load.wait()

    def total_of(taps, n):
        total = taps[0]
        for k in range(1, n):
            total = total + taps[k]
        return total

    ax_total, co_total, ro_total = total_of(ax_s, 64), total_of(co_s, 31), total_of(ro_s, 31)
    span = ROWS + 2 * HALO
    group = iota((16, 256), 1) // 16
    for g in range(8):
        masks[g] = jnp.where(group < 8, jnp.where(group == (g + 7) % 8, 1.0, 0.0), jnp.where(group == g + 8, 1.0, 0.0)).astype(BF16)
    for way in range(2):
        sign = 1 if way == 0 else -1
        shape = (ROWS, span)
        step = iota(shape, 1) - HALO - iota(shape, 0)
        high, low = split(pick(ro_s, 31, sign * step + 15) / ro_total)
        band_d[way] = jnp.concatenate([
            jnp.concatenate([high, high], axis=1), jnp.concatenate([low, jnp.zeros(shape, BF16)], axis=1)], axis=0)

        shape = (16, COLS)

        @pl.loop(0, 16)
        def _(b):
            start = pl.multiple_of(b * 16, 16)
            step = start + iota(shape, 0) - iota(shape, 1)
            high, low = split(pick(co_s, 31, sign * step + 15) / co_total)
            band_w[way, 0, pl.ds(start, 16), :] = high
            band_w[way, 1, pl.ds(start, 16), :] = low
        step = iota(shape, 0) - HALO - iota(shape, 1)
        left_band = split(pick(co_s, 31, sign * step + 15) / co_total)
        step = iota(shape, 0) + COLS - iota(shape, 1)
        right_band = split(pick(co_s, 31, sign * step + 15) / co_total)
        for part in range(2):
            for g in range(8):
                band_w[way, part, 256 + 16 * g:272 + 16 * g, :] = left_band[part]
                band_w[way, part, 384 + 16 * g:400 + 16 * g, :] = right_band[part]

        @pl.loop(0, 16)
        def _(b):
            start = pl.multiple_of(b * 16, 16)
            i = start + iota(shape, 0)
            j = iota(shape, 1)
            step = j // 8 - i // 8
            index = jnp.where(i % 8 == j % 8, sign * step + 32, -1)
            high, low = split(pick(ax_s, 64, index) / ax_total)
            band_a[way, pl.ds(start, 16), :] = jnp.concatenate([high, high, low], axis=1)

    first, last = pl.ds(0, HALO), pl.ds(ROWS - HALO, HALO)
    own = pl.ds(HALO, ROWS)
    before, after = pl.ds(0, HALO), pl.ds(HALO + ROWS, HALO)

    def row_copies(e, volume, planes):
        return [
            (UP, volume.at[planes, first, :], down.at[e, planes], -1, 0),
            (DOWN, volume.at[planes, last, :], up.at[e, planes], 1, 0),
        ]

    def side_copies(e, h):
        return [
            (LEFT, send_left.at[e, h], right.at[e, h, own, :], 0, -1),
            (RIGHT, send_right.at[e, h], left.at[e, h, own, :], 0, 1),
            (LEFT_UP, send_left.at[e, h, first, :], right.at[e, h, after, :], -1, -1),
            (LEFT_DOWN, send_left.at[e, h, last, :], right.at[e, h, before, :], 1, -1),
            (RIGHT_UP, send_right.at[e, h, first, :], left.at[e, h, after, :], -1, 1),
            (RIGHT_DOWN, send_right.at[e, h, last, :], left.at[e, h, before, :], 1, 1),
        ]

    def descriptor(e, h, way, source, target, d_block, d_x):
        return pltpu.make_async_remote_copy(
            src_ref=source, dst_ref=target, send_sem=e_send.at[e, way], recv_sem=e_recv.at[e, h, way],
            device_id=place(d_block, d_x), device_id_type=MESH)

    def chunk(h):
        return pl.ds(8 * h, 8)

    def start(e, h, copies):
        for c in copies:
            pl.when(inside(c[3], c[4]))(descriptor(e, h, *c).start)

    def arrive(e, h, volume):
        for c in row_copies(e, volume, chunk(h)) + side_copies(e, h):
            comes = inside(-c[3], -c[4])
            pl.when(comes)(descriptor(e, h, *c).wait_recv)
            @pl.when(jnp.logical_not(comes))
            def _():
                c[2][...] = jnp.zeros(c[2].shape, F32)

    def drain(e, volume):
        every = slice(None)
        for c in row_copies(e, volume, every) + side_copies(e, every):
            pl.when(inside(c[3], c[4]))(descriptor(e, 0, *c).wait_send)

    lane = iota((ROWS, 128), 1)

    def pack(e, h, volume):
        packed_left = jnp.zeros((ROWS, 128), F32)
        packed_right = jnp.zeros((ROWS, 128), F32)
        for g in range(8):
            ends = jnp.where(lane < 64, volume[8 * h + g, :, 0:128], volume[8 * h + g, :, 128:256])
            if g:
                ends = pltpu.roll(ends, 16 * g, 1)
            packed_left = jnp.where(lane // 16 == g, ends, packed_left)
            packed_right = jnp.where(lane // 16 == (g + 7) % 8, ends, packed_right)
        send_left[e, h] = packed_left
        send_right[e, h] = packed_right

    def along_rows(way, values):
        high, low = split(values)
        both = dot(band_d[way], jnp.concatenate([high, low], axis=0))
        return split(both[:ROWS] + both[ROWS:])

    def lateral(e, way, volume, h):
        strip = along_rows(way, jnp.concatenate([left[e, h], right[e, h]], axis=1))
        for g in range(8):
            plane = 8 * h + g
            high, low = along_rows(way, jnp.concatenate([up[e, plane], volume[plane], down[e, plane]], axis=0))
            here = pl.ds(ROWS * g, ROWS)
            parts[here, 0:256] = high
            parts[here, 256:512] = low
            for part in range(2):
                kept = strip[part].reshape(4, 16, 256) * masks[g][None]
                parts[here, 512 + 256 * part:768 + 256 * part] = kept.reshape(ROWS, 256)
        high, low = parts[:, 0:256], parts[:, 256:512]
        side_high, side_low = parts[:, 512:768], parts[:, 768:1024]
        values = jnp.concatenate([high, side_high, low, side_low, high, side_high], axis=1)
        bands = jnp.concatenate([band_w[way, 0], band_w[way, 0], band_w[way, 1]], axis=0)
        return dot(values, bands).reshape(8, ROWS, COLS)

    def axial(b):
        where = pl.ds(8 * b, 8)

        def product(way, value):
            high, low = split(value)
            return dot(band_a[way], jnp.concatenate([high, low, high], axis=0))

        blurred = product(0, mid[:, where, :].reshape(256, COLS))
        quotient = data[:, where, :].reshape(256, COLS) / (blurred + BACKGROUND)
        quo[:, where, :] = product(1, quotient).reshape(PLANES, 8, COLS)

    def axial_and_send(e):
        for b in (0, 1, 6, 7):
            axial(b)

        @pl.loop(0, 4)
        def _(h):
            start(e, h, row_copies(e, quo, chunk(h)))
        for b in (2, 3, 4, 5):
            axial(b)

        @pl.loop(0, 4)
        def _(h):
            pack(e, h, quo)
            start(e, h, side_copies(e, h))

    def send(e, h, volume):
        start(e, h, row_copies(e, volume, chunk(h)))
        pack(e, h, volume)
        start(e, h, side_copies(e, h))

    def forward(e, h):
        arrive(e, h, est)
        mid[chunk(h)] = lateral(e, 0, est, h)

    def backward(e, h):
        arrive(e, h, quo)
        est[chunk(h)] = est[chunk(h)] * lateral(e, 1, quo, h)

    def turn(o):
        return (ring + o + o // 2 - 2 * (o // 3)) % 4

    @pl.loop(0, 4)
    def _(o):
        h = turn(o)
        for g in range(8):
            plane = 8 * h + g
            base = plane_base(plane)
            here = jnp.logical_and(jnp.logical_and(scan >= base - 1, scan <= base + 6), scan <= LAST_TILE)
            @pl.when(here)
            def _():
                pltpu.make_async_copy(data.at[plane], data.at[plane], d_recv.at[plane]).wait()
            @pl.when(jnp.logical_not(here))
            def _():
                data[plane] = jnp.zeros((ROWS, COLS), F32)
            est[plane] = data[plane] + 1.0
        send(0, h, est)

    @pl.loop(0, 4)
    def _(o):
        forward(0, turn(o))

    axial_and_send(1)
    drain(0, est)

    @pl.loop(0, 4)
    def _(h):
        backward(1, h)
        send(2, h, est)

    @pl.loop(0, 4)
    def _(h):
        forward(2, h)

    drain(1, quo)
    axial_and_send(3)
    drain(2, est)

    columns = pl.ds(pl.multiple_of(256 * x, 256), 256)

    def swap_copies(i, planes):
        owner = 4 * core + i
        source = est.at[planes, pl.ds(16 * i, 16), :]
        target = out.at[planes, :, columns]
        remote = pltpu.make_async_remote_copy(
            src_ref=source, dst_ref=target, send_sem=t_send.at[i], recv_sem=t_recv.at[x],
            device_id=(scan, owner), device_id_type=MESH)
        return owner == row, (source, target, t_recv.at[x]), remote

    @pl.loop(0, 4)
    def _(h):
        backward(3, h)
        for i in range(4):
            here, local, remote = swap_copies(i, chunk(h))
            @pl.when(here)
            def _():
                pltpu.make_async_copy(*local).start()
            pl.when(jnp.logical_not(here))(remote.start)

    drain(3, quo)
    for n in range(2):
        for i in range(12):
            for j in range(4):
                _, _, is_remote, remote = deskew_copies(n, i, j)
                pl.when(is_remote)(remote.wait_send)
    for i in range(4):
        target = out.at[:, :, pl.ds(256 * i, 256)]
        pltpu.make_async_copy(target, target, t_recv.at[i]).wait()
    for i in range(4):
        here, _, remote = swap_copies(i, slice(None))
        pl.when(jnp.logical_not(here))(remote.wait_send)


def shards(raw_planes, shear_tiles, axial_kernel, column_kernel, row_kernel):
    raw = raw_planes.reshape(2, TILES, 16, 1024)
    hbm = pl.BlockSpec(memory_space=pltpu.HBM)
    half = (ITERS * 2, PLANES, HALO, COLS)
    strip = (ITERS * 2, 4, ROWS + 2 * HALO, 128)
    volume = pltpu.VMEM((PLANES, ROWS, COLS), F32)
    out = pl.pallas_call(
        body,
        out_shape=jax.ShapeDtypeStruct((PLANES, 16, 1024), F32),
        in_specs=[hbm] * 5,
        out_specs=pl.BlockSpec(memory_space=pl.ANY),
        scratch_shapes=[
            pltpu.VMEM((2, TILES, 16, 1024), F32),
            pltpu.SMEM((2,), jnp.int32),
            pltpu.SMEM((64,), F32),
            pltpu.SMEM((31,), F32),
            pltpu.SMEM((31,), F32),
            pltpu.VMEM((2, WINDOW, 16, 1024), F32),
            volume, volume, volume, volume,
            pltpu.VMEM(half, F32),
            pltpu.VMEM(half, F32),
            pltpu.VMEM(strip, F32),
            pltpu.VMEM(strip, F32),
            pltpu.VMEM((ITERS * 2, 4, ROWS, 128), F32),
            pltpu.VMEM((ITERS * 2, 4, ROWS, 128), F32),
            pltpu.VMEM((2, 2 * ROWS, 2 * (ROWS + 2 * HALO)), BF16),
            pltpu.VMEM((2, 2, 512, COLS), BF16),
            pltpu.VMEM((2, 256, 768), BF16),
            pltpu.VMEM((8, 16, 256), BF16),
            pltpu.VMEM((8 * ROWS, 1024), BF16),
            pltpu.SemaphoreType.DMA((6,)),
            pltpu.SemaphoreType.DMA((2, 12, 4)),
            pltpu.SemaphoreType.DMA((PLANES,)),
            pltpu.SemaphoreType.DMA((ITERS * 2, 8)),
            pltpu.SemaphoreType.DMA((ITERS * 2, 4, 8)),
            pltpu.SemaphoreType.DMA((4,)),
            pltpu.SemaphoreType.DMA((4,)),
        ],
        compiler_params=pltpu.CompilerParams(collective_id=0, has_side_effects=True, vmem_limit_bytes=60 << 20),
        name="deconvolve",
    )(raw, shear_tiles, axial_kernel, column_kernel, row_kernel)
    return out.reshape(PLANES, 1, 16, 1024)


def solution(mesh):
    return jax.shard_map(
        shards,
        mesh=mesh,
        in_specs=(P("scan", None, "row", None), P("scan"), P(), P(), P()),
        out_specs=P(None, "scan", "row", None),
        check_vma=False,
    )
```

```python
import jax
import jax.numpy as jnp
from jax import lax
from jax.experimental import pallas as pl
from jax.experimental.pallas import tpu as pltpu
from jax.sharding import PartitionSpec as P

PLANES = 32
TILES = 6
WINDOW = 8
LAST_TILE = 10
ROWS = 64
COLS = 256
HALO = 16
INSIDE = ROWS - 2 * HALO
ITERS = 2
BACKGROUND = 0.5
F32 = jnp.float32
BF16 = jnp.bfloat16
MESH = pl.DeviceIdType.MESH
UP, DOWN, LEFT, RIGHT, LEFT_UP, LEFT_DOWN, RIGHT_UP, RIGHT_DOWN = range(8)


def split(value):
    high = value.astype(BF16)
    low = (value - high.astype(F32)).astype(BF16)
    return high, low


def dot(a, b):
    return jnp.dot(a, b, preferred_element_type=F32)


def iota(shape, axis):
    return lax.broadcasted_iota(jnp.int32, shape, axis)


def pick(taps, count, index):
    value = jnp.zeros(index.shape, F32)
    for tap in range(count):
        value = jnp.where(index == tap, taps[tap], value)
    return value


def plane_base(plane):
    return (plane * 5) // 31


def body(raw_in, shear_in, ax_in, co_in, ro_in, out,
         raw, shear, ax_s, co_s, ro_s, win, data, est, quo, mid, up, down, left, right, send_left, send_right,
         band_d, band_i, band_e, band_w, band_a, masks, parts,
         in_sem, d_send, d_recv, e_send, e_recv, t_send, t_recv):
    scan = lax.axis_index("scan")
    row = lax.axis_index("row")
    x = row // 2
    core = row % 2
    block = 2 * scan + core
    half = x // 2
    ring = scan // 4

    loads = [pltpu.make_async_copy(a, b, in_sem.at[i]) for i, (a, b) in enumerate(
        [(shear_in, shear), (raw_in.at[0], raw.at[0]), (raw_in.at[1], raw.at[1]), (ax_in, ax_s), (co_in, co_s), (ro_in, ro_s)])]
    for load in loads:
        load.start()

    barrier = pltpu.get_barrier_semaphore()

    def inside(d_block, d_x):
        return jnp.logical_and(jnp.logical_and(block + d_block >= 0, block + d_block < 32),
                               jnp.logical_and(x + d_x >= 0, x + d_x < 4))

    def place(d_block, d_x):
        other = block + d_block
        return (other // 2, 2 * (x + d_x) + other % 2)

    def greet(condition, device):
        @pl.when(condition)
        def _():
            pl.semaphore_signal(barrier, inc=1, device_id=device, device_id_type=MESH)

    def window(source):
        first = plane_base(2 * source) - 1
        last = plane_base(2 * source + 1) + 6
        return jnp.maximum(first, 0), jnp.minimum(last, LAST_TILE)

    @pl.loop(0, 16)
    def _(source):
        first, last = window(source)
        sends = jnp.logical_and(scan >= first, scan <= last)
        for i in range(4):
            other = 4 * core + i
            greet(jnp.logical_and(sends, jnp.logical_or(source != scan, other != row)), (source, other))

    count = 0
    for d_block in (-1, 0, 1):
        for d_x in (-1, 0, 1):
            if d_block or d_x:
                greet(inside(d_block, d_x), place(d_block, d_x))
                count = count + inside(d_block, d_x).astype(jnp.int32)
    for i in range(4):
        other = 2 * i + row // 4
        greet(other != row, (scan, other))
    first, last = window(scan)
    count = count + 4 * (last - first + 1)
    to_self = jnp.logical_and(jnp.logical_and(scan >= first, scan <= last), half == core)
    count = count - to_self.astype(jnp.int32)
    count = count + 4 - (row // 4 == core).astype(jnp.int32)

    loads[0].wait()
    for n in range(2):
        loads[1 + n].wait()
        delta = shear[n] - plane_base(2 * scan + n)
        for k in range(WINDOW):
            zero = jnp.zeros(raw.shape[2:], F32)
            early = raw[n, k] if k < TILES else zero
            level = raw[n, k - 1] if 1 <= k <= TILES else zero
            late = raw[n, k - 2] if k >= 2 else zero
            win[n, k] = jnp.where(delta == 0, level, jnp.where(delta < 0, early, late))

    def deskew_copies(n, i, j):
        plane = 2 * scan + n
        base = plane_base(plane)
        tile = 4 * ((1 + ring % 2 + i // 4) % 3) + (i + scan) % 4
        cb = (x + j) % 4
        offset = 32 * (x % 2) + 16 * core
        source = win.at[n, jnp.clip(tile - base + 1, 0, WINDOW - 1), :, pl.ds(pl.multiple_of(256 * cb, 256), 256)]
        target = data.at[plane, pl.ds(pl.multiple_of(offset, 16), 16), :]
        real = jnp.logical_and(jnp.logical_and(tile >= base - 1, tile <= base + 6), tile <= LAST_TILE)
        mine = jnp.logical_and(tile == scan, jnp.logical_and(cb == x, half == core))
        remote = pltpu.make_async_remote_copy(
            src_ref=source, dst_ref=target, send_sem=d_send.at[n, i, j], recv_sem=d_recv.at[plane],
            device_id=(tile, 2 * cb + half), device_id_type=MESH)
        return jnp.logical_and(real, mine), (source, target, d_recv.at[plane]), jnp.logical_and(real, jnp.logical_not(mine)), remote

    pl.semaphore_wait(barrier, count)
    def deskew_sent(items):
        for i in items:
            for n in range(2):
                for j in range(4):
                    _, _, is_remote, remote = deskew_copies(n, i, j)
                    pl.when(is_remote)(remote.wait_send)

    for i in range(12):
        if i == 8:
            deskew_sent(range(4))
        for n in range(2):
            for j in range(4):
                is_local, local, is_remote, remote = deskew_copies(n, i, j)
                if j == 0:
                    @pl.when(is_local)
                    def _():
                        pltpu.make_async_copy(*local).start()
                pl.when(is_remote)(remote.start)

    for load in loads[3:]:
        load.wait()

    def total_of(taps, n):
        total = taps[0]
        for k in range(1, n):
            total = total + taps[k]
        return total

    ax_total, co_total, ro_total = total_of(ax_s, 64), total_of(co_s, 31), total_of(ro_s, 31)
    span = ROWS + 2 * HALO
    group = iota((16, 256), 1) // 16
    for g in range(8):
        masks[g] = jnp.where(group < 8, jnp.where(group == (g + 7) % 8, 1.0, 0.0), jnp.where(group == g + 8, 1.0, 0.0)).astype(BF16)
    for way in range(2):
        sign = 1 if way == 0 else -1
        def rows_band(band, count, width, line):
            shape = (count, width)
            step = iota(shape, 1) - HALO - line(iota(shape, 0))
            high, low = split(pick(ro_s, 31, sign * step + 15) / ro_total)
            band[way] = jnp.concatenate([
                jnp.concatenate([high, high], axis=1), jnp.concatenate([low, jnp.zeros(shape, BF16)], axis=1)], axis=0)

        rows_band(band_d, ROWS, span, lambda i: i)
        rows_band(band_i, INSIDE, ROWS, lambda i: i)
        rows_band(band_e, INSIDE, span, lambda i: jnp.where(i < HALO, i, i + INSIDE))

        shape = (16, COLS)

        @pl.loop(0, 16)
        def _(b):
            start = pl.multiple_of(b * 16, 16)
            step = start + iota(shape, 0) - iota(shape, 1)
            high, low = split(pick(co_s, 31, sign * step + 15) / co_total)
            band_w[way, 0, pl.ds(start, 16), :] = high
            band_w[way, 1, pl.ds(start, 16), :] = low
        step = iota(shape, 0) - HALO - iota(shape, 1)
        left_band = split(pick(co_s, 31, sign * step + 15) / co_total)
        step = iota(shape, 0) + COLS - iota(shape, 1)
        right_band = split(pick(co_s, 31, sign * step + 15) / co_total)
        for part in range(2):
            for g in range(8):
                band_w[way, part, 256 + 16 * g:272 + 16 * g, :] = left_band[part]
                band_w[way, part, 384 + 16 * g:400 + 16 * g, :] = right_band[part]

        @pl.loop(0, 16)
        def _(b):
            start = pl.multiple_of(b * 16, 16)
            i = start + iota(shape, 0)
            j = iota(shape, 1)
            step = j // 8 - i // 8
            index = jnp.where(i % 8 == j % 8, sign * step + 32, -1)
            high, low = split(pick(ax_s, 64, index) / ax_total)
            band_a[way, pl.ds(start, 16), :] = jnp.concatenate([high, high, low], axis=1)

    first, last = pl.ds(0, HALO), pl.ds(ROWS - HALO, HALO)
    own = pl.ds(HALO, ROWS)
    before, after = pl.ds(0, HALO), pl.ds(HALO + ROWS, HALO)

    def row_copies(e, volume, planes):
        return [
            (UP, volume.at[planes, first, :], down.at[e, planes], -1, 0),
            (DOWN, volume.at[planes, last, :], up.at[e, planes], 1, 0),
        ]

    def side_copies(e, h):
        return [
            (LEFT, send_left.at[e, h], right.at[e, h, own, :], 0, -1),
            (RIGHT, send_right.at[e, h], left.at[e, h, own, :], 0, 1),
            (LEFT_UP, send_left.at[e, h, first, :], right.at[e, h, after, :], -1, -1),
            (LEFT_DOWN, send_left.at[e, h, last, :], right.at[e, h, before, :], 1, -1),
            (RIGHT_UP, send_right.at[e, h, first, :], left.at[e, h, after, :], -1, 1),
            (RIGHT_DOWN, send_right.at[e, h, last, :], left.at[e, h, before, :], 1, 1),
        ]

    def descriptor(e, h, way, source, target, d_block, d_x):
        return pltpu.make_async_remote_copy(
            src_ref=source, dst_ref=target, send_sem=e_send.at[e, way], recv_sem=e_recv.at[e, h, way],
            device_id=place(d_block, d_x), device_id_type=MESH)

    def chunk(h):
        return pl.ds(8 * h, 8)

    def start(e, h, copies):
        for c in copies:
            pl.when(inside(c[3], c[4]))(descriptor(e, h, *c).start)

    def arrive(e, h, copies):
        for c in copies:
            comes = inside(-c[3], -c[4])
            pl.when(comes)(descriptor(e, h, *c).wait_recv)
            @pl.when(jnp.logical_not(comes))
            def _():
                c[2][...] = jnp.zeros(c[2].shape, F32)

    def drain(e, volume):
        every = slice(None)
        for c in row_copies(e, volume, every) + side_copies(e, every):
            pl.when(inside(c[3], c[4]))(descriptor(e, 0, *c).wait_send)

    lane = iota((ROWS, 128), 1)

    def pack(e, h, volume):
        packed_left = jnp.zeros((ROWS, 128), F32)
        packed_right = jnp.zeros((ROWS, 128), F32)
        for g in range(8):
            ends = jnp.where(lane < 64, volume[8 * h + g, :, 0:128], volume[8 * h + g, :, 128:256])
            if g:
                ends = pltpu.roll(ends, 16 * g, 1)
            packed_left = jnp.where(lane // 16 == g, ends, packed_left)
            packed_right = jnp.where(lane // 16 == (g + 7) % 8, ends, packed_right)
        send_left[e, h] = packed_left
        send_right[e, h] = packed_right

    def along_rows(band, values):
        high, low = split(values)
        both = dot(band, jnp.concatenate([high, low], axis=0))
        count = both.shape[0] // 2
        return split(both[:count] + both[count:])

    ALL, MIDDLE, EDGES = (band_d, ROWS, True), (band_i, INSIDE, False), (band_e, INSIDE, True)

    def lateral(e, way, volume, h, kind):
        band, count, halo = kind
        strip_rows = slice(None) if halo else own
        strip = along_rows(band[way], jnp.concatenate([left[e, h, strip_rows], right[e, h, strip_rows]], axis=1))
        for g in range(8):
            plane = 8 * h + g
            values = volume[plane]
            if halo:
                values = jnp.concatenate([up[e, plane], values, down[e, plane]], axis=0)
            high, low = along_rows(band[way], values)
            here = pl.ds(count * g, count)
            parts[here, 0:256] = high
            parts[here, 256:512] = low
            for part in range(2):
                kept = strip[part].reshape(count // 16, 16, 256) * masks[g][None]
                parts[here, 512 + 256 * part:768 + 256 * part] = kept.reshape(count, 256)
        used = pl.ds(0, 8 * count)
        high, low = parts[used, 0:256], parts[used, 256:512]
        side_high, side_low = parts[used, 512:768], parts[used, 768:1024]
        values = jnp.concatenate([high, side_high, low, side_low, high, side_high], axis=1)
        bands = jnp.concatenate([band_w[way, 0], band_w[way, 0], band_w[way, 1]], axis=0)
        return dot(values, bands).reshape(8, count, COLS)

    def axial(b):
        where = pl.ds(8 * b, 8)

        def product(way, value):
            high, low = split(value)
            return dot(band_a[way], jnp.concatenate([high, low, high], axis=0))

        blurred = product(0, mid[:, where, :].reshape(256, COLS))
        quotient = data[:, where, :].reshape(256, COLS) / (blurred + BACKGROUND)
        quo[:, where, :] = product(1, quotient).reshape(PLANES, 8, COLS)

    middle = pl.ds(HALO, INSIDE)

    def axial_and_send(e, rows_first):
        def send_rows():
            for h in range(4):
                start(e, h, row_copies(e, quo, chunk(h)))

        for b in (0, 1, 6, 7):
            axial(b)
        if rows_first:
            send_rows()
        for b in (2, 3, 4, 5):
            axial(b)
        for h in range(4):
            pack(e, h, quo)
            start(e, h, side_copies(e, h))
        if not rows_first:
            send_rows()

    def send(e, h, volume):
        start(e, h, row_copies(e, volume, chunk(h)))
        pack(e, h, volume)
        start(e, h, side_copies(e, h))

    def forward(e, h):
        arrive(e, h, row_copies(e, est, chunk(h)) + side_copies(e, h))
        mid[chunk(h)] = lateral(e, 0, est, h, ALL)

    def backward(e, h):
        arrive(e, h, row_copies(e, quo, chunk(h)) + side_copies(e, h))
        est[chunk(h)] = est[chunk(h)] * lateral(e, 1, quo, h, ALL)

    def backward_middle(e, h):
        arrive(e, h, side_copies(e, h)[:2])
        est[chunk(h), middle] = est[chunk(h), middle] * lateral(e, 1, quo, h, MIDDLE)

    def backward_edges(e, h):
        arrive(e, h, row_copies(e, quo, chunk(h)) + side_copies(e, h)[2:])
        value = lateral(e, 1, quo, h, EDGES)
        est[chunk(h), first] = est[chunk(h), first] * value[:, :HALO]
        est[chunk(h), last] = est[chunk(h), last] * value[:, HALO:]

    def turn(o):
        return (ring + o + o // 2 - 2 * (o // 3)) % 4

    @pl.loop(0, 4)
    def _(o):
        h = turn(o)
        for g in range(8):
            plane = 8 * h + g
            base = plane_base(plane)
            here = jnp.logical_and(jnp.logical_and(scan >= base - 1, scan <= base + 6), scan <= LAST_TILE)
            @pl.when(here)
            def _():
                pltpu.make_async_copy(data.at[plane], data.at[plane], d_recv.at[plane]).wait()
            @pl.when(jnp.logical_not(here))
            def _():
                data[plane] = jnp.zeros((ROWS, COLS), F32)
            est[plane] = data[plane] + 1.0
        send(0, h, est)

    @pl.loop(0, 4)
    def _(o):
        forward(0, turn(o))

    axial_and_send(1, True)
    drain(0, est)

    @pl.loop(0, 4)
    def _(h):
        backward(1, h)
        send(2, h, est)

    @pl.loop(0, 4)
    def _(h):
        forward(2, h)

    drain(1, quo)
    axial_and_send(3, False)
    drain(2, est)

    columns = pl.ds(pl.multiple_of(256 * x, 256), 256)

    def swap_copies(i, planes):
        owner = 4 * core + i
        source = est.at[planes, pl.ds(16 * i, 16), :]
        target = out.at[planes, :, columns]
        remote = pltpu.make_async_remote_copy(
            src_ref=source, dst_ref=target, send_sem=t_send.at[i], recv_sem=t_recv.at[x],
            device_id=(scan, owner), device_id_type=MESH)
        return owner == row, (source, target, t_recv.at[x]), remote

    def swap(h, pieces):
        for i in pieces:
            here, local, remote = swap_copies(i, chunk(h))
            @pl.when(here)
            def _():
                pltpu.make_async_copy(*local).start()
            pl.when(jnp.logical_not(here))(remote.start)

    @pl.loop(0, 4)
    def _(h):
        backward_middle(3, h)
        swap(h, (1, 2))

    @pl.loop(0, 4)
    def _(h):
        backward_edges(3, h)
        swap(h, (0, 3))

    drain(3, quo)
    deskew_sent(range(4, 12))
    for i in range(4):
        target = out.at[:, :, pl.ds(256 * i, 256)]
        pltpu.make_async_copy(target, target, t_recv.at[i]).wait()
    for i in range(4):
        here, _, remote = swap_copies(i, slice(None))
        pl.when(jnp.logical_not(here))(remote.wait_send)


def shards(raw_planes, shear_tiles, axial_kernel, column_kernel, row_kernel):
    raw = raw_planes.reshape(2, TILES, 16, 1024)
    operands = (raw, shear_tiles, axial_kernel, column_kernel, row_kernel)
    hbm = pl.BlockSpec(memory_space=pltpu.HBM)
    half = (ITERS * 2, PLANES, HALO, COLS)
    strip = (ITERS * 2, 4, ROWS + 2 * HALO, 128)
    volume = pltpu.VMEM((PLANES, ROWS, COLS), F32)
    out = pl.pallas_call(
        body,
        out_shape=jax.ShapeDtypeStruct((PLANES, 16, 1024), F32),
        in_specs=[hbm] * 5,
        out_specs=pl.BlockSpec(memory_space=pl.ANY),
        scratch_shapes=[
            pltpu.VMEM((2, TILES, 16, 1024), F32),
            pltpu.SMEM((2,), jnp.int32),
            pltpu.SMEM((64,), F32),
            pltpu.SMEM((31,), F32),
            pltpu.SMEM((31,), F32),
            pltpu.VMEM((2, WINDOW, 16, 1024), F32),
            volume, volume, volume, volume,
            pltpu.VMEM(half, F32),
            pltpu.VMEM(half, F32),
            pltpu.VMEM(strip, F32),
            pltpu.VMEM(strip, F32),
            pltpu.VMEM((ITERS * 2, 4, ROWS, 128), F32),
            pltpu.VMEM((ITERS * 2, 4, ROWS, 128), F32),
            pltpu.VMEM((2, 2 * ROWS, 2 * (ROWS + 2 * HALO)), BF16),
            pltpu.VMEM((2, 2 * INSIDE, 2 * ROWS), BF16),
            pltpu.VMEM((2, 2 * INSIDE, 2 * (ROWS + 2 * HALO)), BF16),
            pltpu.VMEM((2, 2, 512, COLS), BF16),
            pltpu.VMEM((2, 256, 768), BF16),
            pltpu.VMEM((8, 16, 256), BF16),
            pltpu.VMEM((8 * ROWS, 1024), BF16),
            pltpu.SemaphoreType.DMA((6,)),
            pltpu.SemaphoreType.DMA((2, 12, 4)),
            pltpu.SemaphoreType.DMA((PLANES,)),
            pltpu.SemaphoreType.DMA((ITERS * 2, 8)),
            pltpu.SemaphoreType.DMA((ITERS * 2, 4, 8)),
            pltpu.SemaphoreType.DMA((4,)),
            pltpu.SemaphoreType.DMA((4,)),
        ],
        compiler_params=pltpu.CompilerParams(collective_id=0, has_side_effects=True, vmem_limit_bytes=48 << 20),
        name="deconvolve",
    )(*(pltpu.with_memory_space_constraint(a, pltpu.HBM) for a in operands))
    return out.reshape(PLANES, 1, 16, 1024)


def solution(mesh):
    return jax.shard_map(
        shards,
        mesh=mesh,
        in_specs=(P("scan", None, "row", None), P("scan"), P(), P(), P()),
        out_specs=P(None, "scan", "row", None),
        check_vma=False,
    )
```

```python
import jax
import jax.numpy as jnp
from jax import lax
from jax.experimental import pallas as pl
from jax.experimental.pallas import tpu as pltpu
from jax.sharding import PartitionSpec as P

PLANES = 32
TILES = 6
WINDOW = 8
LAST_TILE = 10
ROWS = 64
COLS = 256
HALO = 16
INSIDE = ROWS - 2 * HALO
ITERS = 2
BACKGROUND = 0.5
F32 = jnp.float32
BF16 = jnp.bfloat16
MESH = pl.DeviceIdType.MESH
UP, DOWN, LEFT, RIGHT, LEFT_UP, LEFT_DOWN, RIGHT_UP, RIGHT_DOWN = range(8)


def split(value):
    high = value.astype(BF16)
    low = (value - high.astype(F32)).astype(BF16)
    return high, low


def dot(a, b):
    return jnp.dot(a, b, preferred_element_type=F32)


def iota(shape, axis):
    return lax.broadcasted_iota(jnp.int32, shape, axis)


def pick(taps, count, index):
    value = jnp.zeros(index.shape, F32)
    for tap in range(count):
        value = jnp.where(index == tap, taps[tap], value)
    return value


def plane_base(plane):
    return (plane * 5) // 31


def body(raw_in, shear_in, ax_in, co_in, ro_in, out,
         raw, shear, ax_s, co_s, ro_s, win, data, est, quo, mid, up, down, left, right, send_left, send_right,
         band_d, band_i, band_e, band_w, band_a, masks, parts,
         in_sem, d_send, d_recv, e_send, e_recv, t_send, t_recv):
    scan = lax.axis_index("scan")
    row = lax.axis_index("row")
    x = row // 2
    core = row % 2
    block = 2 * scan + core
    half = x // 2
    ring = scan // 4

    loads = [pltpu.make_async_copy(a, b, in_sem.at[i]) for i, (a, b) in enumerate(
        [(shear_in, shear), (raw_in.at[0], raw.at[0]), (raw_in.at[1], raw.at[1]), (ax_in, ax_s), (co_in, co_s), (ro_in, ro_s)])]
    for load in loads:
        load.start()

    barrier = pltpu.get_barrier_semaphore()

    def inside(d_block, d_x):
        return jnp.logical_and(jnp.logical_and(block + d_block >= 0, block + d_block < 32),
                               jnp.logical_and(x + d_x >= 0, x + d_x < 4))

    def place(d_block, d_x):
        other = block + d_block
        return (other // 2, 2 * (x + d_x) + other % 2)

    def greet(condition, device):
        @pl.when(condition)
        def _():
            pl.semaphore_signal(barrier, inc=1, device_id=device, device_id_type=MESH)

    def window(source):
        first = plane_base(2 * source) - 1
        last = plane_base(2 * source + 1) + 6
        return jnp.maximum(first, 0), jnp.minimum(last, LAST_TILE)

    @pl.loop(0, 16)
    def _(source):
        first, last = window(source)
        sends = jnp.logical_and(scan >= first, scan <= last)
        for i in range(4):
            other = 4 * core + i
            greet(jnp.logical_and(sends, jnp.logical_or(source != scan, other != row)), (source, other))

    count = 0
    for d_block in (-1, 0, 1):
        for d_x in (-1, 0, 1):
            if d_block or d_x:
                greet(inside(d_block, d_x), place(d_block, d_x))
                count = count + inside(d_block, d_x).astype(jnp.int32)
    for i in range(4):
        other = 2 * i + row // 4
        greet(other != row, (scan, other))
    first, last = window(scan)
    count = count + 4 * (last - first + 1)
    to_self = jnp.logical_and(jnp.logical_and(scan >= first, scan <= last), half == core)
    count = count - to_self.astype(jnp.int32)
    count = count + 4 - (row // 4 == core).astype(jnp.int32)

    loads[0].wait()
    for n in range(2):
        loads[1 + n].wait()
        delta = shear[n] - plane_base(2 * scan + n)
        for k in range(WINDOW):
            zero = jnp.zeros(raw.shape[2:], F32)
            early = raw[n, k] if k < TILES else zero
            level = raw[n, k - 1] if 1 <= k <= TILES else zero
            late = raw[n, k - 2] if k >= 2 else zero
            win[n, k] = jnp.where(delta == 0, level, jnp.where(delta < 0, early, late))

    def deskew_copies(n, i, j):
        plane = 2 * scan + n
        base = plane_base(plane)
        tile = 4 * ((1 + ring % 2 + i // 4) % 3) + (i + scan) % 4
        cb = (x + j) % 4
        offset = 32 * (x % 2) + 16 * core
        source = win.at[n, jnp.clip(tile - base + 1, 0, WINDOW - 1), :, pl.ds(pl.multiple_of(256 * cb, 256), 256)]
        target = data.at[plane, pl.ds(pl.multiple_of(offset, 16), 16), :]
        real = jnp.logical_and(jnp.logical_and(tile >= base - 1, tile <= base + 6), tile <= LAST_TILE)
        mine = jnp.logical_and(tile == scan, jnp.logical_and(cb == x, half == core))
        remote = pltpu.make_async_remote_copy(
            src_ref=source, dst_ref=target, send_sem=d_send.at[n, i, j], recv_sem=d_recv.at[plane],
            device_id=(tile, 2 * cb + half), device_id_type=MESH)
        return jnp.logical_and(real, mine), (source, target, d_recv.at[plane]), jnp.logical_and(real, jnp.logical_not(mine)), remote

    pl.semaphore_wait(barrier, count)
    def deskew_sent(items):
        for i in items:
            for n in range(2):
                for j in range(4):
                    _, _, is_remote, remote = deskew_copies(n, i, j)
                    pl.when(is_remote)(remote.wait_send)

    for i in range(12):
        if i == 8:
            deskew_sent(range(2))
        for n in range(2):
            for j in range(4):
                is_local, local, is_remote, remote = deskew_copies(n, i, j)
                if j == 0:
                    @pl.when(is_local)
                    def _():
                        pltpu.make_async_copy(*local).start()
                pl.when(is_remote)(remote.start)

    for load in loads[3:]:
        load.wait()

    def total_of(taps, n):
        total = taps[0]
        for k in range(1, n):
            total = total + taps[k]
        return total

    ax_total, co_total, ro_total = total_of(ax_s, 64), total_of(co_s, 31), total_of(ro_s, 31)
    span = ROWS + 2 * HALO
    group = iota((16, 256), 1) // 16
    for g in range(8):
        masks[g] = jnp.where(group < 8, jnp.where(group == (g + 7) % 8, 1.0, 0.0), jnp.where(group == g + 8, 1.0, 0.0)).astype(BF16)
    for way in range(2):
        sign = 1 if way == 0 else -1
        def rows_band(band, count, width, line):
            shape = (count, width)
            step = iota(shape, 1) - HALO - line(iota(shape, 0))
            high, low = split(pick(ro_s, 31, sign * step + 15) / ro_total)
            band[way] = jnp.concatenate([
                jnp.concatenate([high, high], axis=1), jnp.concatenate([low, jnp.zeros(shape, BF16)], axis=1)], axis=0)

        rows_band(band_d, ROWS, span, lambda i: i)
        rows_band(band_i, INSIDE, ROWS, lambda i: i)
        rows_band(band_e, INSIDE, span, lambda i: jnp.where(i < HALO, i, i + INSIDE))

        shape = (16, COLS)

        @pl.loop(0, 16)
        def _(b):
            start = pl.multiple_of(b * 16, 16)
            step = start + iota(shape, 0) - iota(shape, 1)
            high, low = split(pick(co_s, 31, sign * step + 15) / co_total)
            band_w[way, 0, pl.ds(start, 16), :] = high
            band_w[way, 1, pl.ds(start, 16), :] = low
        step = iota(shape, 0) - HALO - iota(shape, 1)
        left_band = split(pick(co_s, 31, sign * step + 15) / co_total)
        step = iota(shape, 0) + COLS - iota(shape, 1)
        right_band = split(pick(co_s, 31, sign * step + 15) / co_total)
        for part in range(2):
            for g in range(8):
                band_w[way, part, 256 + 16 * g:272 + 16 * g, :] = left_band[part]
                band_w[way, part, 384 + 16 * g:400 + 16 * g, :] = right_band[part]

        @pl.loop(0, 16)
        def _(b):
            start = pl.multiple_of(b * 16, 16)
            i = start + iota(shape, 0)
            j = iota(shape, 1)
            step = j // 8 - i // 8
            index = jnp.where(i % 8 == j % 8, sign * step + 32, -1)
            high, low = split(pick(ax_s, 64, index) / ax_total)
            band_a[way, pl.ds(start, 16), :] = jnp.concatenate([high, high, low], axis=1)

    first, last = pl.ds(0, HALO), pl.ds(ROWS - HALO, HALO)
    own = pl.ds(HALO, ROWS)
    before, after = pl.ds(0, HALO), pl.ds(HALO + ROWS, HALO)

    def row_copies(e, volume, planes):
        return [
            (UP, volume.at[planes, first, :], down.at[e, planes], -1, 0),
            (DOWN, volume.at[planes, last, :], up.at[e, planes], 1, 0),
        ]

    def side_copies(e, h):
        return [
            (LEFT, send_left.at[e, h], right.at[e, h, own, :], 0, -1),
            (RIGHT, send_right.at[e, h], left.at[e, h, own, :], 0, 1),
            (LEFT_UP, send_left.at[e, h, first, :], right.at[e, h, after, :], -1, -1),
            (LEFT_DOWN, send_left.at[e, h, last, :], right.at[e, h, before, :], 1, -1),
            (RIGHT_UP, send_right.at[e, h, first, :], left.at[e, h, after, :], -1, 1),
            (RIGHT_DOWN, send_right.at[e, h, last, :], left.at[e, h, before, :], 1, 1),
        ]

    def descriptor(e, h, way, source, target, d_block, d_x):
        return pltpu.make_async_remote_copy(
            src_ref=source, dst_ref=target, send_sem=e_send.at[e, way], recv_sem=e_recv.at[e, h, way],
            device_id=place(d_block, d_x), device_id_type=MESH)

    def chunk(h):
        return pl.ds(8 * h, 8)

    def start(e, h, copies):
        for c in copies:
            pl.when(inside(c[3], c[4]))(descriptor(e, h, *c).start)

    def arrive(e, h, copies):
        for c in copies:
            comes = inside(-c[3], -c[4])
            pl.when(comes)(descriptor(e, h, *c).wait_recv)
            @pl.when(jnp.logical_not(comes))
            def _():
                c[2][...] = jnp.zeros(c[2].shape, F32)

    def drain(e, volume):
        every = slice(None)
        for c in row_copies(e, volume, every) + side_copies(e, every):
            pl.when(inside(c[3], c[4]))(descriptor(e, 0, *c).wait_send)

    lane = iota((ROWS, 128), 1)

    def pack(e, h, volume):
        packed_left = jnp.zeros((ROWS, 128), F32)
        packed_right = jnp.zeros((ROWS, 128), F32)
        for g in range(8):
            ends = jnp.where(lane < 64, volume[8 * h + g, :, 0:128], volume[8 * h + g, :, 128:256])
            if g:
                ends = pltpu.roll(ends, 16 * g, 1)
            packed_left = jnp.where(lane // 16 == g, ends, packed_left)
            packed_right = jnp.where(lane // 16 == (g + 7) % 8, ends, packed_right)
        send_left[e, h] = packed_left
        send_right[e, h] = packed_right

    def along_rows(band, values):
        high, low = split(values)
        both = dot(band, jnp.concatenate([high, low], axis=0))
        count = both.shape[0] // 2
        return both[:count] + both[count:]

    ALL, MIDDLE, EDGES = (band_d, ROWS, True), (band_i, INSIDE, False), (band_e, INSIDE, True)

    def lateral(e, way, volume, h, kind):
        band, count, halo = kind
        strip_rows = slice(None) if halo else own
        strip = along_rows(band[way], jnp.concatenate([left[e, h, strip_rows], right[e, h, strip_rows]], axis=1))
        side_high = strip.astype(BF16).reshape(count // 16, 16, 256)
        rest = strip - strip.astype(BF16).astype(F32)
        rest = jnp.concatenate([pltpu.roll(rest[:, :128], 16, 1), pltpu.roll(rest[:, 128:], 16, 1)], axis=1)
        side_low = rest.astype(BF16).reshape(count // 16, 16, 256)
        for g in range(8):
            plane = 8 * h + g
            values = volume[plane]
            if halo:
                values = jnp.concatenate([up[e, plane], values, down[e, plane]], axis=0)
            high, low = split(along_rows(band[way], values))
            here = pl.ds(count * g, count)
            parts[here, 0:256] = high
            parts[here, 256:512] = low
            kept = side_high * masks[g][None]
            both = kept + side_low * masks[(g + 1) % 8][None]
            parts[here, 512:768] = kept.reshape(count, 256)
            parts[here, 768:1024] = both.reshape(count, 256)
        used = pl.ds(0, 8 * count)
        high, low = parts[used, 0:256], parts[used, 256:512]
        side_high, side_both = parts[used, 512:768], parts[used, 768:1024]
        values = jnp.concatenate([low, high, side_both, high, side_high], axis=1)
        bands = jnp.concatenate([band_w[way, 0, 0:COLS, :], band_w[way, 0], band_w[way, 1]], axis=0)
        return dot(values, bands).reshape(8, count, COLS)

    def axial(b):
        where = pl.ds(8 * b, 8)

        def product(way, value):
            high, low = split(value)
            return dot(band_a[way], jnp.concatenate([high, low, high], axis=0))

        blurred = product(0, mid[:, where, :].reshape(256, COLS))
        quotient = data[:, where, :].reshape(256, COLS) / (blurred + BACKGROUND)
        quo[:, where, :] = product(1, quotient).reshape(PLANES, 8, COLS)

    middle = pl.ds(HALO, INSIDE)

    def axial_and_send(e, rows_first):
        def send_rows():
            for h in range(4):
                start(e, h, row_copies(e, quo, chunk(h)))

        for b in (0, 1, 6, 7):
            axial(b)
        if rows_first:
            send_rows()
        for b in (2, 3, 4, 5):
            axial(b)
        for h in range(4):
            pack(e, h, quo)
            start(e, h, side_copies(e, h))
        if not rows_first:
            send_rows()

    def send(e, h, volume):
        start(e, h, row_copies(e, volume, chunk(h)))
        pack(e, h, volume)
        start(e, h, side_copies(e, h))

    def forward(e, h):
        arrive(e, h, row_copies(e, est, chunk(h)) + side_copies(e, h))
        mid[chunk(h)] = lateral(e, 0, est, h, ALL)

    def backward(e, h):
        arrive(e, h, row_copies(e, quo, chunk(h)) + side_copies(e, h))
        est[chunk(h)] = est[chunk(h)] * lateral(e, 1, quo, h, ALL)

    def backward_middle(e, h):
        arrive(e, h, side_copies(e, h)[:2])
        est[chunk(h), middle] = est[chunk(h), middle] * lateral(e, 1, quo, h, MIDDLE)

    def backward_edges(e, h):
        arrive(e, h, row_copies(e, quo, chunk(h)) + side_copies(e, h)[2:])
        value = lateral(e, 1, quo, h, EDGES)
        est[chunk(h), first] = est[chunk(h), first] * value[:, :HALO]
        est[chunk(h), last] = est[chunk(h), last] * value[:, HALO:]

    def turn(o):
        return (ring + o + o // 2 - 2 * (o // 3)) % 4

    @pl.loop(0, 4)
    def _(o):
        h = turn(o)
        for g in range(8):
            plane = 8 * h + g
            base = plane_base(plane)
            here = jnp.logical_and(jnp.logical_and(scan >= base - 1, scan <= base + 6), scan <= LAST_TILE)
            @pl.when(here)
            def _():
                pltpu.make_async_copy(data.at[plane], data.at[plane], d_recv.at[plane]).wait()
            @pl.when(jnp.logical_not(here))
            def _():
                data[plane] = jnp.zeros((ROWS, COLS), F32)
            est[plane] = data[plane] + 1.0
        send(0, h, est)

    @pl.loop(0, 4)
    def _(o):
        forward(0, turn(o))

    axial_and_send(1, True)
    drain(0, est)

    @pl.loop(0, 4)
    def _(h):
        backward(1, h)
        send(2, h, est)

    @pl.loop(0, 4)
    def _(h):
        forward(2, h)

    drain(1, quo)
    axial_and_send(3, False)
    drain(2, est)

    columns = pl.ds(pl.multiple_of(256 * x, 256), 256)

    def swap_copies(i, planes):
        owner = 4 * core + i
        source = est.at[planes, pl.ds(16 * i, 16), :]
        target = out.at[planes, :, columns]
        remote = pltpu.make_async_remote_copy(
            src_ref=source, dst_ref=target, send_sem=t_send.at[i], recv_sem=t_recv.at[x],
            device_id=(scan, owner), device_id_type=MESH)
        return owner == row, (source, target, t_recv.at[x]), remote

    def swap(h, pieces):
        for i in pieces:
            here, local, remote = swap_copies(i, chunk(h))
            @pl.when(here)
            def _():
                pltpu.make_async_copy(*local).start()
            pl.when(jnp.logical_not(here))(remote.start)

    @pl.loop(0, 4)
    def _(h):
        backward_middle(3, h)
        swap(h, (1, 2))

    @pl.loop(0, 4)
    def _(h):
        backward_edges(3, h)
        swap(h, (0, 3))

    drain(3, quo)
    deskew_sent(range(2, 12))
    for i in range(4):
        target = out.at[:, :, pl.ds(256 * i, 256)]
        pltpu.make_async_copy(target, target, t_recv.at[i]).wait()
    for i in range(4):
        here, _, remote = swap_copies(i, slice(None))
        pl.when(jnp.logical_not(here))(remote.wait_send)


def shards(raw_planes, shear_tiles, axial_kernel, column_kernel, row_kernel):
    raw = raw_planes.reshape(2, TILES, 16, 1024)
    operands = (raw, shear_tiles, axial_kernel, column_kernel, row_kernel)
    hbm = pl.BlockSpec(memory_space=pltpu.HBM)
    half = (ITERS * 2, PLANES, HALO, COLS)
    strip = (ITERS * 2, 4, ROWS + 2 * HALO, 128)
    volume = pltpu.VMEM((PLANES, ROWS, COLS), F32)
    out = pl.pallas_call(
        body,
        out_shape=jax.ShapeDtypeStruct((PLANES, 16, 1024), F32),
        in_specs=[hbm] * 5,
        out_specs=pl.BlockSpec(memory_space=pl.ANY),
        scratch_shapes=[
            pltpu.VMEM((2, TILES, 16, 1024), F32),
            pltpu.SMEM((2,), jnp.int32),
            pltpu.SMEM((64,), F32),
            pltpu.SMEM((31,), F32),
            pltpu.SMEM((31,), F32),
            pltpu.VMEM((2, WINDOW, 16, 1024), F32),
            volume, volume, volume, volume,
            pltpu.VMEM(half, F32),
            pltpu.VMEM(half, F32),
            pltpu.VMEM(strip, F32),
            pltpu.VMEM(strip, F32),
            pltpu.VMEM((ITERS * 2, 4, ROWS, 128), F32),
            pltpu.VMEM((ITERS * 2, 4, ROWS, 128), F32),
            pltpu.VMEM((2, 2 * ROWS, 2 * (ROWS + 2 * HALO)), BF16),
            pltpu.VMEM((2, 2 * INSIDE, 2 * ROWS), BF16),
            pltpu.VMEM((2, 2 * INSIDE, 2 * (ROWS + 2 * HALO)), BF16),
            pltpu.VMEM((2, 2, 512, COLS), BF16),
            pltpu.VMEM((2, 256, 768), BF16),
            pltpu.VMEM((8, 16, 256), BF16),
            pltpu.VMEM((8 * ROWS, 1024), BF16),
            pltpu.SemaphoreType.DMA((6,)),
            pltpu.SemaphoreType.DMA((2, 12, 4)),
            pltpu.SemaphoreType.DMA((PLANES,)),
            pltpu.SemaphoreType.DMA((ITERS * 2, 8)),
            pltpu.SemaphoreType.DMA((ITERS * 2, 4, 8)),
            pltpu.SemaphoreType.DMA((4,)),
            pltpu.SemaphoreType.DMA((4,)),
        ],
        compiler_params=pltpu.CompilerParams(collective_id=0, has_side_effects=True, vmem_limit_bytes=48 << 20),
        name="deconvolve",
    )(*(pltpu.with_memory_space_constraint(a, pltpu.HBM) for a in operands))
    return out.reshape(PLANES, 1, 16, 1024)


def solution(mesh):
    return jax.shard_map(
        shards,
        mesh=mesh,
        in_specs=(P("scan", None, "row", None), P("scan"), P(), P(), P()),
        out_specs=P(None, "scan", "row", None),
        check_vma=False,
    )
```
